32 devices in a mesh: dp: 8 (over y, x, core), seq: 4 (over z).
Axes of the slice: x: 2, y: 2, z: 4, core: 2. Of those that a mesh axis runs over, the one named last changes fastest.
Arguments:
- video: bfloat16 [8, 512, 3072], P('dp', 'seq'), may hold values from -6 to 6
- cotangent: bfloat16 [8, 512, 3072], P('dp', 'seq'), may hold values from -6 to 6
- w_query: bfloat16 [3072, 3072], P(None, 'seq'), may hold values from -0.109375 to 0.109375
- w_out: bfloat16 [3072, 3072], P('seq'), may hold values from -0.109375 to 0.109375
- ref_kv: bfloat16 [8, 2, 1024, 3072], P('dp', None, 'seq'), may hold values from -400 to 400, as said below
- tile_lists: int32 [8, 2, 4, 3], P('dp'), may hold values from -1 to 3, as said below
Outputs:
- output: bfloat16 [8, 512, 3072], P('dp', 'seq')
- grad_video: bfloat16 [8, 512, 3072], P('dp', 'seq')
- grad_wq: float32 [3072, 3072], P(None, 'seq')
- grad_wo: float32 [3072, 3072], P('seq')
- grad_ref: bfloat16 [8, 2, 1024, 3072], P('dp', None, 'seq')
The draws below stay inside these ranges and needn't reach their ends.
Inputs may be any that keep to these rules, and one draw needn't show every extreme that they name: `ref_kv`: values are of order one; key rows may carry scales of up to some tens. `tile_lists`: each row lists first 1 to 3 different tile indices from 0 to 3, consecutive modulo 4, then -1; the first video tile of every clip lists exactly 3 tiles for each person.
All inputs are finite; a program needn't handle non-finite values.
Results may differ from the reference program's by a relative error of at most 0.012.
The reference program's roundings to bfloat16 on the way (of `query`, `probs`, `attention`, `grad_attention`, `grad_scores` and `grad_query`) count: a program that leaves them out, or rounds other values in their place, can miss the bound.
Values may be sent and summed in bfloat16 or wider, within the bound.
No kernel may reach another device: no remote copies, remote signals or barrier semaphores. Data moves between devices by JAX's collectives and lax.ppermute only.
A program may use at most 128 MiB of HBM per device.

```python
import math
import jax
import jax.numpy as jnp
from jax import lax

HEADS = 24
HD = 128
D = 3072
REF = 512
PERSONS = 2
TILE = 128
LMAX = 3
CLIPS = 8
TOKENS = 512
VT = 4
RT = 4
N_SEQ = 4


def draw_ref_kv(key, part):
    base_key = jax.random.fold_in(key, 11)
    dims = (CLIPS, 2, PERSONS * REF, D)
    values = jnp.clip(jax.random.normal(base_key, dims, jnp.float32), -6.0, 6.0)
    return values.astype(jnp.bfloat16)


def draw_tile_lists(key, part):
    start_key = jax.random.fold_in(key, 21)
    count_key = jax.random.fold_in(key, 22)
    first = jax.random.randint(start_key, (CLIPS, PERSONS, VT, 1), 0, RT)
    counts = jax.random.randint(count_key, (CLIPS, PERSONS, VT, 1), 1, LMAX + 1)
    counts = counts.at[:, :, 0, :].set(LMAX)
    places = jnp.arange(LMAX, dtype=jnp.int32)
    return jnp.where(places < counts, (first + places) % RT, -1).astype(jnp.int32)


def block_scale(key, shape, cuts, least, top_value):
    loudness = 1.0
    for position, blocks in cuts:
        heights = jax.random.uniform(jax.random.fold_in(jax.random.fold_in(key, 6), position), (blocks,), jnp.float32, least / len(cuts), top_value / len(cuts))
        loudness = loudness * jnp.repeat(jnp.exp(heights), shape[position] // blocks).reshape((-1,) + (1,) * (len(shape) - 1 - position))
    return loudness


def gaussian(stream_key, shape, spread, limit, shards=(), kind=jnp.bfloat16):
    gain = block_scale(stream_key, shape, shards, -0.22, 0.18) if shards else 1.0
    values = jax.random.normal(stream_key, shape, jnp.float32) * spread * gain
    return jnp.minimum(jnp.maximum(values, -limit), limit).astype(kind)


def setup_inputs(seed: int = 0) -> dict:
    key_list = jax.random.split(jax.random.key(seed), 7)
    return {
        "video": gaussian(key_list[0], (CLIPS, TOKENS, D), 1.0, 6.0, ((0, 8), (1, 4))),
        "cotangent": gaussian(key_list[1], (CLIPS, TOKENS, D), 1.0, 6.0, ((0, 8), (1, 4))),
        "w_query": gaussian(key_list[2], (D, D), D ** -0.5, 0.109375, ((1, 4),)),
        "w_out": gaussian(key_list[3], (D, D), D ** -0.5, 0.109375, ((0, 4),)),
        "ref_kv": draw_ref_kv(jax.random.fold_in(key_list[6], 71), 0),
        "tile_lists": draw_tile_lists(jax.random.fold_in(key_list[6], 71), 0),
    }


def build_allowed(tile_lists, tile_size, ref_tokens):
    tiles_each = ref_tokens // tile_size
    matched = jnp.any(tile_lists[..., None] == jnp.arange(tiles_each, dtype=jnp.int32), axis=-2)
    tile_table = jnp.transpose(matched, (1, 0, 2)).reshape(matched.shape[1], -1)
    return jnp.repeat(jnp.repeat(tile_table, tile_size, axis=0), tile_size, axis=1)

def split_heads(array, heads_count):
    return jnp.transpose(array.reshape(array.shape[0], heads_count, -1), (1, 0, 2))

def merge_heads(array):
    return jnp.transpose(array, (1, 0, 2)).reshape(array.shape[1], -1)

def softmax_weights(query, keys, allowed, score_scale):
    scores = jnp.dot(query, keys.T, preferred_element_type=jnp.float32) * score_scale
    scores = jnp.where(allowed, scores, -1e+30)
    peak = lax.optimization_barrier(jnp.max(scores, axis=-1, keepdims=True))
    weights = jnp.exp(scores - peak)
    return weights / lax.optimization_barrier(jnp.sum(weights, axis=-1, keepdims=True))

def head_forward(query, keys, values, allowed, score_scale):
    weights = softmax_weights(query, keys, allowed, score_scale)
    probs = weights.astype(jnp.bfloat16)
    return jnp.dot(probs, values, preferred_element_type=jnp.float32).astype(jnp.bfloat16)

def head_backward(query, keys, values, grad_out, allowed, score_scale):
    weights = softmax_weights(query, keys, allowed, score_scale)
    probs = weights.astype(jnp.bfloat16)
    grad_probs = jnp.dot(grad_out, values.T, preferred_element_type=jnp.float32)
    delta = lax.optimization_barrier(jnp.sum(grad_probs * weights, axis=-1, keepdims=True))
    grad_scores = (weights * (grad_probs - delta) * score_scale).astype(jnp.bfloat16)
    grad_query = jnp.dot(grad_scores, keys, preferred_element_type=jnp.float32).astype(jnp.bfloat16)
    grad_keys = jnp.dot(grad_scores.T, query, preferred_element_type=jnp.float32).astype(jnp.bfloat16)
    grad_values = jnp.dot(probs.T, grad_out, preferred_element_type=jnp.float32).astype(jnp.bfloat16)
    return (grad_query, grad_keys, grad_values)

def rounded(value):
    return lax.optimization_barrier(value.astype(jnp.bfloat16)).astype(jnp.float32)

def reference(video, cotangent, w_query, w_out, ref_kv, tile_lists):
    score_scale = 1.0 / math.sqrt(HD)
    group_width = D // N_SEQ

    def one_clip(carry, inputs):
        sum_wq, sum_wo = carry
        clip_video, clip_grad, clip_kv, clip_lists = inputs
        query = jnp.dot(clip_video, w_query, preferred_element_type=jnp.float32).astype(jnp.bfloat16)
        allowed = build_allowed(clip_lists, TILE, REF)
        q_heads = split_heads(query, HEADS)
        k_heads = split_heads(clip_kv[0], HEADS)
        v_heads = split_heads(clip_kv[1], HEADS)
        attn_heads = lax.map(lambda item: head_forward(item[0], item[1], item[2], allowed, score_scale), (q_heads, k_heads, v_heads))
        attention = merge_heads(attn_heads)
        output = jnp.dot(attention, w_out, preferred_element_type=jnp.float32).astype(jnp.bfloat16)
        grad_attention = jnp.dot(clip_grad, w_out.T, preferred_element_type=jnp.float32).astype(jnp.bfloat16)
        grad_wo = jnp.dot(attention.T, clip_grad, preferred_element_type=jnp.float32)
        back = lax.map(lambda item: head_backward(item[0], item[1], item[2], item[3], allowed, score_scale), (q_heads, k_heads, v_heads, split_heads(grad_attention, HEADS)))
        grad_query = merge_heads(back[0])
        grad_ref = jnp.stack([merge_heads(back[1]), merge_heads(back[2])])
        grad_video = jnp.zeros(clip_video.shape, jnp.float32)
        for group in range(N_SEQ):
            columns = slice(group * group_width, (group + 1) * group_width)
            part_sum = jnp.dot(grad_query[:, columns], w_query[:, columns].T, preferred_element_type=jnp.float32)
            grad_video = grad_video + rounded(part_sum)
        grad_wq = jnp.dot(clip_video.T, grad_query, preferred_element_type=jnp.float32)
        carry = (sum_wq + rounded(grad_wq), sum_wo + rounded(grad_wo))
        return (carry, (output, grad_video.astype(jnp.bfloat16), grad_ref))
    start = (jnp.zeros((D, D), jnp.float32), jnp.zeros((D, D), jnp.float32))
    sums, results = lax.scan(one_clip, start, (video, cotangent, ref_kv, tile_lists))
    return (results[0], results[1], sums[0], sums[1], results[2])
```

```python
import functools
import math

import jax
import jax.numpy as jnp
from jax import lax
from jax.experimental import pallas as pl
from jax.experimental.pallas import tpu as pltpu
from jax.sharding import PartitionSpec as P

HD = 128
TILE = 128
F32 = jnp.float32
BF16 = jnp.bfloat16
NEG = -1e30


def contract_last(left, right):
    return lax.dot_general(left, right, (((1,), (1,)), ((), ())), preferred_element_type=F32)


def contract_first(left, right):
    return lax.dot_general(left, right, (((0,), (0,)), ((), ())), preferred_element_type=F32)


def tile_table(tile_lists, ref_tiles, me, n):
    matched = jnp.any(tile_lists[..., None] == jnp.arange(ref_tiles, dtype=jnp.int32), axis=-2)
    table = jnp.transpose(matched, (1, 0, 2)).reshape(matched.shape[1], -1).astype(jnp.int32)
    source = lax.rem(me - jnp.arange(n, dtype=jnp.int32) + n, n)
    table = table.reshape(n, -1, table.shape[1])[source].reshape(table.shape)
    return table.reshape(table.shape[0], n, -1)[:, source].reshape(table.shape)


def masked(scores, table_ref, row, first, scale, axis):
    tiles = []
    for t in range(scores.shape[axis] // TILE):
        part = lax.slice_in_dim(scores, t * TILE, (t + 1) * TILE, axis=axis) * scale
        tiles.append(jnp.where(table_ref[row, first + t] != 0, part, NEG))
    return tiles


def forward_kernel(n, scale, table_ref, q_ref, *refs):
    kv_refs, out_ref = refs[:n], refs[n]
    local = kv_refs[0].shape[1] // TILE
    for i in range(q_ref.shape[0] // TILE):
        rows = pl.ds(i * TILE, TILE)
        query = q_ref[rows, :]
        scores = []
        for k in range(n):
            scores += masked(contract_last(query, kv_refs[k][0]), table_ref, i, k * local, scale, 1)
        peak = functools.reduce(jnp.maximum, scores)
        peak = jnp.max(peak, axis=1, keepdims=True)
        powers = [jnp.exp(s - peak) for s in scores]
        total = jnp.sum(functools.reduce(jnp.add, powers), axis=1, keepdims=True)
        inverse = 1.0 / total
        probs = [(p * inverse).astype(BF16) for p in powers]
        acc = None
        for k in range(n):
            part = jnp.concatenate(probs[k * local : (k + 1) * local], axis=1)
            part = jnp.dot(part, kv_refs[k][1], preferred_element_type=F32)
            acc = part if acc is None else acc + part
        out_ref[rows, :] = acc.astype(BF16)


def backward_kernel(n, scale, table_ref, q_ref, g_ref, *refs):
    kv_refs, dq_ref, dkv_refs = refs[:n], refs[n], refs[n + 1 : 2 * n + 1]
    probs_ref, dscores_ref = refs[2 * n + 1 :]
    length = kv_refs[0].shape[1]
    local = length // TILE
    for i in range(q_ref.shape[0] // TILE):
        rows = pl.ds(i * TILE, TILE)
        query, grad = q_ref[rows, :], g_ref[rows, :]
        scores, dprobs = [], []
        for k in range(n):
            scores += masked(contract_last(kv_refs[k][0], query), table_ref, i, k * local, scale, 0)
        peak = functools.reduce(jnp.maximum, scores)
        peak = jnp.max(peak, axis=0, keepdims=True)
        powers = [jnp.exp(s - peak) for s in scores]
        total = jnp.sum(functools.reduce(jnp.add, powers), axis=0, keepdims=True)
        inverse = 1.0 / total
        weights = [p * inverse for p in powers]
        for k in range(n):
            part = contract_last(kv_refs[k][1], grad)
            dprobs += [part[t * TILE : (t + 1) * TILE] for t in range(local)]
        delta = functools.reduce(jnp.add, [d * w for d, w in zip(dprobs, weights)])
        delta = jnp.sum(delta, axis=0, keepdims=True)
        for j in range(n * local):
            keys = pl.ds(j * TILE, TILE)
            probs_ref[keys, rows] = weights[j].astype(BF16)
            dscores_ref[keys, rows] = (weights[j] * (dprobs[j] - delta) * scale).astype(BF16)
    dq = None
    for k in range(n):
        keys = pl.ds(k * length, length)
        dscores = dscores_ref[keys, :]
        dkv_refs[k][0] = jnp.dot(dscores, q_ref[...], preferred_element_type=F32).astype(BF16)
        dkv_refs[k][1] = jnp.dot(probs_ref[keys, :], g_ref[...], preferred_element_type=F32).astype(BF16)
        part = contract_first(kv_refs[k][0], dscores)
        dq = part if dq is None else dq + part
    dq_ref[...] = dq.T.astype(BF16)


def attend(table, query, pieces, scale):
    n = len(pieces)
    tokens, width = query.shape
    length = pieces[0].shape[1]
    rows = pl.BlockSpec((tokens, HD), lambda h, t: (0, h))
    piece = pl.BlockSpec((2, length, HD), lambda h, t: (0, 0, h))
    work = tokens * n * length * width
    return pl.pallas_call(
        functools.partial(forward_kernel, n, scale),
        out_shape=jax.ShapeDtypeStruct(query.shape, BF16),
        grid_spec=pltpu.PrefetchScalarGridSpec(
            num_scalar_prefetch=1,
            grid=(width // HD,),
            in_specs=[rows] + [piece] * n,
            out_specs=rows,
        ),
        cost_estimate=pl.CostEstimate(
            flops=4 * work, transcendentals=work // HD, bytes_accessed=4 * width * (tokens + n * length)
        ),
        compiler_params=pltpu.CompilerParams(vmem_limit_bytes=48 << 20),
    )(table, query, *pieces)


def attend_back(table, query, grad, pieces, scale, first, heads):
    n = len(pieces)
    tokens = query.shape[0]
    length = pieces[0].shape[1]
    width = heads * HD
    rows = pl.BlockSpec((tokens, HD), lambda h, t: (0, first + h))
    piece = pl.BlockSpec((2, length, HD), lambda h, t: (0, 0, first + h))
    work = tokens * n * length * width
    return pl.pallas_call(
        functools.partial(backward_kernel, n, scale),
        out_shape=[jax.ShapeDtypeStruct((tokens, width), BF16)]
        + [jax.ShapeDtypeStruct((2, length, width), BF16)] * n,
        grid_spec=pltpu.PrefetchScalarGridSpec(
            num_scalar_prefetch=1,
            grid=(heads,),
            in_specs=[rows, rows] + [piece] * n,
            out_specs=[pl.BlockSpec((tokens, HD), lambda h, t: (0, h))]
            + [pl.BlockSpec((2, length, HD), lambda h, t: (0, 0, h))] * n,
            scratch_shapes=[pltpu.VMEM((n * length, tokens), BF16)] * 2,
        ),
        cost_estimate=pl.CostEstimate(
            flops=10 * work, transcendentals=work // HD, bytes_accessed=2 * width * (3 * tokens + 4 * n * length)
        ),
        compiler_params=pltpu.CompilerParams(vmem_limit_bytes=48 << 20),
    )(table, query, grad, *pieces)


def shift(array, n, by):
    return lax.ppermute(array, "seq", [(i, (i + by) % n) for i in range(n)])


def line_gather(block, n, me):
    right, left = [block], [block]
    for s in range(1, n):
        right.append(lax.ppermute(right[-1], "seq", [(i, i + 1) for i in range(s - 1, n - 1)]))
        left.append(lax.ppermute(left[-1], "seq", [(i, i - 1) for i in range(1, n - s + 1)]))
    parts = [block] + [jnp.where(me >= k, right[k], left[n - k]) for k in range(1, n)]
    return jnp.concatenate(parts, axis=0)


def line_scatter(partial, n):
    size = partial.shape[0] // n
    parts = [partial[k * size : (k + 1) * size].astype(F32) for k in range(n)]
    right = left = None
    for s in range(1, n):
        to_right = parts[s] if right is None else parts[s] + right.astype(F32)
        to_left = parts[n - s] if left is None else parts[n - s] + left.astype(F32)
        right = lax.ppermute(to_right.astype(BF16), "seq", [(i, i + 1) for i in range(s)])
        left = lax.ppermute(to_left.astype(BF16), "seq", [(i, i - 1) for i in range(n - s, n)])
    return (parts[0] + right.astype(F32) + left.astype(F32)).astype(BF16)


def body(video, cotangent, w_query, w_out, ref_kv, tile_lists):
    n = lax.axis_size("seq")
    me = lax.axis_index("seq")
    width = w_query.shape[1]
    heads = width // HD
    chunks = 3 if heads % 3 == 0 else 1
    length = ref_kv.shape[2]
    ref_tiles = length * n // TILE // tile_lists.shape[1]
    scale = 1.0 / math.sqrt(HD)
    table = tile_table(tile_lists[0], ref_tiles, me, n)

    gathered = line_gather(video[0], n, me)
    pieces = []
    for k in range(n):
        columns = lax.rem(me + k, n) * width
        piece = lax.dynamic_slice_in_dim(ref_kv[0], columns, width, axis=2)
        pieces.append(piece if k == 0 else shift(piece, n, k))
    query = jnp.dot(gathered, w_query, preferred_element_type=F32).astype(BF16)
    attention = attend(table, query, pieces, scale)

    late = lax.optimization_barrier((cotangent[0], *pieces[1:]))[0]
    grad_rows = line_gather(late, n, me)
    output = line_scatter(jnp.dot(attention, w_out, preferred_element_type=F32), n)

    grad_attention = contract_last(grad_rows, w_out).astype(BF16)
    grad_wo = contract_first(attention, grad_rows).astype(BF16)
    grad_wo = lax.psum(grad_wo, "dp").astype(F32)

    grad_ref = jnp.zeros(ref_kv.shape[1:], BF16)
    grad_query = []
    per = heads // chunks
    for c in range(chunks):
        back = attend_back(table, query, grad_attention, pieces, scale, c * per, per)
        grad_query.append(back[0])
        for k in range(n):
            block = back[1 + k] if k == 0 else shift(back[1 + k], n, -k)
            columns = lax.rem(me + k, n) * width + c * per * HD
            grad_ref = lax.dynamic_update_slice_in_dim(grad_ref, block, columns, axis=2)
    grad_query = jnp.concatenate(grad_query, axis=1)
    grad_video = line_scatter(contract_last(grad_query, w_query).astype(BF16), n)
    grad_wq = contract_first(gathered, grad_query).astype(BF16)
    grad_wq = lax.psum(grad_wq, "dp").astype(F32)
    return (output[None], grad_video[None], grad_wq, grad_wo, grad_ref[None])


def solution(mesh):
    in_specs = (
        P("dp", "seq", None),
        P("dp", "seq", None),
        P(None, "seq"),
        P("seq", None),
        P("dp", None, "seq", None),
        P("dp", None, None, None),
    )
    out_specs = (
        P("dp", "seq", None),
        P("dp", "seq", None),
        P(None, "seq"),
        P("seq", None),
        P("dp", None, "seq", None),
    )
    return jax.shard_map(body, mesh=mesh, in_specs=in_specs, out_specs=out_specs, check_vma=False)
```

```python
import functools
import math

import jax
import jax.numpy as jnp
from jax import lax
from jax.experimental import pallas as pl
from jax.experimental.pallas import tpu as pltpu
from jax.sharding import PartitionSpec as P

HD = 128
TILE = 128
F32 = jnp.float32
BF16 = jnp.bfloat16
NEG = -1e30


def contract_last(left, right):
    return lax.dot_general(left, right, (((1,), (1,)), ((), ())), preferred_element_type=F32)


def contract_first(left, right):
    return lax.dot_general(left, right, (((0,), (0,)), ((), ())), preferred_element_type=F32)


def tile_table(tile_lists, ref_tiles, me, n):
    matched = jnp.any(tile_lists[..., None] == jnp.arange(ref_tiles, dtype=jnp.int32), axis=-2)
    table = jnp.transpose(matched, (1, 0, 2)).reshape(matched.shape[1], -1).astype(jnp.int32)
    source = lax.rem(me - jnp.arange(n, dtype=jnp.int32) + n, n)
    table = table.reshape(n, -1, table.shape[1])[source].reshape(table.shape)
    return table.reshape(table.shape[0], n, -1)[:, source].reshape(table.shape)


def masked(scores, table_ref, row, first, scale, axis):
    tiles = []
    for t in range(scores.shape[axis] // TILE):
        part = lax.slice_in_dim(scores, t * TILE, (t + 1) * TILE, axis=axis) * scale
        tiles.append(jnp.where(table_ref[row, first + t] != 0, part, NEG))
    return tiles


def forward_kernel(n, scale, table_ref, q_ref, *refs):
    kv_refs, out_ref = refs[:n], refs[n]
    local = kv_refs[0].shape[1] // TILE
    wide = math.gcd(q_ref.shape[0] // TILE, 4)

    def block(i, carry):
        rows = pl.ds(pl.multiple_of(i * wide * TILE, TILE), wide * TILE)
        query = q_ref[rows, :]
        scores = []
        for k in range(n):
            part = contract_last(kv_refs[k][0], query)
            for t in range(local):
                tiles = []
                for j in range(wide):
                    tile = part[t * TILE : (t + 1) * TILE, j * TILE : (j + 1) * TILE] * scale
                    tiles.append(jnp.where(table_ref[i * wide + j, k * local + t] != 0, tile, NEG))
                scores.append(jnp.concatenate(tiles, axis=1))
        peak = jnp.max(functools.reduce(jnp.maximum, scores), axis=0, keepdims=True)
        powers = [jnp.exp(s - peak) for s in scores]
        total = jnp.sum(functools.reduce(jnp.add, powers), axis=0, keepdims=True)
        inverse = 1.0 / total
        probs = [(p * inverse).astype(BF16) for p in powers]
        acc = None
        for k in range(n):
            part = jnp.concatenate(probs[k * local : (k + 1) * local], axis=0)
            part = contract_first(kv_refs[k][1], part)
            acc = part if acc is None else acc + part
        out_ref[rows, :] = acc.T.astype(BF16)
        return carry

    lax.fori_loop(0, q_ref.shape[0] // TILE // wide, block, 0)


def backward_kernel(n, scale, table_ref, source_ref, q_ref, g_ref, *refs):
    kv_refs, (dq_ref, dkv_ref, probs_ref, dscores_ref) = refs[:n], refs[-4:]
    length = kv_refs[0].shape[1]
    local = length // TILE

    wide = math.gcd(q_ref.shape[0] // TILE, 4)

    def block(i, carry):
        rows = pl.ds(pl.multiple_of(i * wide * TILE, TILE), wide * TILE)
        query, grad = q_ref[rows, :], g_ref[rows, :]
        scores, dprobs = [], []
        for k in range(n):
            part = contract_last(kv_refs[k][0], query)
            for t in range(local):
                tiles = []
                for j in range(wide):
                    tile = part[t * TILE : (t + 1) * TILE, j * TILE : (j + 1) * TILE] * scale
                    tiles.append(jnp.where(table_ref[i * wide + j, k * local + t] != 0, tile, NEG))
                scores.append(jnp.concatenate(tiles, axis=1))
        peak = functools.reduce(jnp.maximum, scores)
        peak = jnp.max(peak, axis=0, keepdims=True)
        powers = [jnp.exp(s - peak) for s in scores]
        total = jnp.sum(functools.reduce(jnp.add, powers), axis=0, keepdims=True)
        inverse = 1.0 / total
        weights = [p * inverse for p in powers]
        for k in range(n):
            part = contract_last(kv_refs[k][1], grad)
            dprobs += [part[t * TILE : (t + 1) * TILE] for t in range(local)]
        delta = functools.reduce(jnp.add, [d * w for d, w in zip(dprobs, weights)])
        delta = jnp.sum(delta, axis=0, keepdims=True)
        for j in range(n * local):
            keys = pl.ds(j * TILE, TILE)
            probs_ref[keys, rows] = weights[j].astype(BF16)
            dscores_ref[keys, rows] = (weights[j] * (dprobs[j] - delta) * scale).astype(BF16)
        return carry

    lax.fori_loop(0, q_ref.shape[0] // TILE // wide, block, 0)
    dq = None
    for k in range(n):
        keys = pl.ds(k * length, length)
        dscores = dscores_ref[keys, :]
        dkv_ref[source_ref[k], 0] = jnp.dot(dscores, q_ref[...], preferred_element_type=F32).astype(BF16)
        dkv_ref[source_ref[k], 1] = jnp.dot(probs_ref[keys, :], g_ref[...], preferred_element_type=F32).astype(BF16)
        part = contract_first(kv_refs[k][0], dscores)
        dq = part if dq is None else dq + part
    dq_ref[...] = dq.T.astype(BF16)


def attend(table, query, pieces, scale, first, heads):
    n = len(pieces)
    tokens = query.shape[0]
    width = heads * HD
    length = pieces[0].shape[1]
    rows = pl.BlockSpec((tokens, HD), lambda h, t: (0, first + h))
    piece = pl.BlockSpec((2, length, HD), lambda h, t: (0, 0, first + h))
    work = tokens * n * length * width
    return pl.pallas_call(
        functools.partial(forward_kernel, n, scale),
        out_shape=jax.ShapeDtypeStruct((tokens, width), BF16),
        grid_spec=pltpu.PrefetchScalarGridSpec(
            num_scalar_prefetch=1,
            grid=(heads,),
            in_specs=[rows] + [piece] * n,
            out_specs=pl.BlockSpec((tokens, HD), lambda h, t: (0, h)),
        ),
        cost_estimate=pl.CostEstimate(
            flops=4 * work, transcendentals=work // HD, bytes_accessed=4 * width * (tokens + n * length)
        ),
        compiler_params=pltpu.CompilerParams(vmem_limit_bytes=48 << 20),
    )(table, query, *pieces)


def attend_back(table, source, query, grad, pieces, scale, first, heads, earlier=()):
    n = len(pieces)
    tokens, width = query.shape
    length = pieces[0].shape[1]
    rows = pl.BlockSpec((tokens, HD), lambda h, t, s: (0, first + h))
    piece = pl.BlockSpec((2, length, HD), lambda h, t, s: (0, 0, first + h))
    work = tokens * n * length * heads * HD
    return pl.pallas_call(
        functools.partial(backward_kernel, n, scale),
        out_shape=[
            jax.ShapeDtypeStruct((tokens, width), BF16),
            jax.ShapeDtypeStruct((n, 2, length, width), BF16),
        ],
        grid_spec=pltpu.PrefetchScalarGridSpec(
            num_scalar_prefetch=2,
            grid=(heads,),
            in_specs=[rows, rows] + [piece] * n + [pl.BlockSpec(memory_space=pl.ANY)] * len(earlier),
            out_specs=[rows, pl.BlockSpec((n, 2, length, HD), lambda h, t, s: (0, 0, 0, first + h))],
            scratch_shapes=[pltpu.VMEM((n * length, tokens), BF16)] * 2,
        ),
        input_output_aliases={4 + n + i: i for i in range(len(earlier))},
        cost_estimate=pl.CostEstimate(
            flops=10 * work,
            transcendentals=work // HD,
            bytes_accessed=2 * heads * HD * (3 * tokens + 4 * n * length),
        ),
        compiler_params=pltpu.CompilerParams(vmem_limit_bytes=48 << 20),
    )(table, source, query, grad, *pieces, *earlier)


def after(array, *others):
    return lax.optimization_barrier((array, *others))[0]


def shift(array, n, by):
    return lax.ppermute(array, "seq", [(i, (i + by) % n) for i in range(n)])


def both_ways(right, left, ups, downs, me):
    up, down = [(i, i + 1) for i in ups], [(i, i - 1) for i in downs]
    apart = not {i for i, _ in up} & {i for i, _ in down} and not {j for _, j in up} & {j for _, j in down}
    if not apart:
        return lax.ppermute(right, "seq", up), lax.ppermute(left, "seq", down)
    rightward = (me >= ups[0]) & (me <= ups[-1])
    came = lax.ppermute(jnp.where(rightward, right, left), "seq", up + down)
    none = jnp.zeros_like(came)
    from_left = (me > ups[0]) & (me <= ups[-1] + 1)
    from_right = (me >= downs[0] - 1) & (me < downs[-1])
    return jnp.where(from_left, came, none), jnp.where(from_right, came, none)


def gather_step(block, state, n, me):
    s = len(state[0]) + 1
    right, left = (side[-1] if side else block for side in state)
    right, left = both_ways(right, left, range(s - 1, n - 1), range(1, n - s + 1), me)
    return (state[0] + [right], state[1] + [left])


def join(block, state, me):
    right, left = state
    others = [jnp.where(me > k, right[k], left[len(left) - 1 - k]) for k in range(len(right))]
    return jnp.concatenate([block] + others, axis=0)


def scatter_step(parts, state, n, me):
    steps, right, left = state
    s = steps + 1
    right = parts[s] if right is None else parts[s] + right.astype(F32)
    left = parts[n - s] if left is None else parts[n - s] + left.astype(F32)
    return s, *both_ways(right.astype(BF16), left.astype(BF16), range(s), range(n - s, n), me)


def split(partial, n):
    size = partial.shape[0] // n
    return [partial[k * size : (k + 1) * size].astype(F32) for k in range(n)]


class ClipSum:
    def __init__(self, array, paths):
        self.size = lax.axis_size("dp")
        self.index = lax.axis_index("dp")
        rows = array.shape[0] // len(paths)
        self.blocks = [array[p * rows : (p + 1) * rows] for p in range(len(paths))]
        self.paths = paths
        self.done = 0

    def exchange(self, block, mask):
        return lax.ppermute(block, "dp", [(i, i ^ mask) for i in range(self.size)])

    def step(self, *others):
        count = len(self.paths[0])
        if self.done == 2 * count:
            return ()
        for p, path in enumerate(self.paths):
            block = self.blocks[p]
            if self.done < count:
                mask = path[self.done]
                high = lax.shift_right_logical(self.index, mask.bit_length() - 1) & 1
                half = block.shape[0] // 2
                give = lax.dynamic_slice_in_dim(block, (1 - high) * half, half).astype(BF16)
                keep = lax.dynamic_slice_in_dim(block, high * half, half).astype(F32)
                self.blocks[p] = keep + self.exchange(after(give, *others), mask).astype(F32)
            else:
                mask = path[2 * count - 1 - self.done]
                high = lax.shift_right_logical(self.index, mask.bit_length() - 1) & 1
                block = after(block.astype(BF16), *others)
                other = self.exchange(block, mask)
                pair = jnp.concatenate([block, other]), jnp.concatenate([other, block])
                self.blocks[p] = jnp.where(high == 0, *pair)
        self.done += 1
        return tuple(self.blocks)

    def result(self):
        while self.done < 2 * len(self.paths[0]):
            self.step()
        return jnp.concatenate(self.blocks).astype(F32)


def body(video, cotangent, w_query, w_out, ref_kv, tile_lists):
    n = lax.axis_size("seq")
    me = lax.axis_index("seq")
    masks = [1 << b for b in range(lax.axis_size("dp").bit_length() - 1)]
    width = w_query.shape[1]
    heads = width // HD
    chunks = 2 if heads % 2 == 0 else 1
    length = ref_kv.shape[2]
    ref_tiles = length * n // TILE // tile_lists.shape[1]
    scale = 1.0 / math.sqrt(HD)
    table = tile_table(tile_lists[0], ref_tiles, me, n)

    pieces = []
    for k in range(n):
        columns = lax.rem(me + k, n) * width
        piece = lax.dynamic_slice_in_dim(ref_kv[0], columns, width, axis=2)
        pieces.append(shift(piece, n, k) if k else piece)
    order = sorted(range(1, n), key=lambda k: (min(k, n - k), -k))
    rows = ([], [])
    for s in range(1, n):
        block = video[0]
        if s > 1:
            rows = tuple(side[:-1] + [after(side[-1], pieces[order[s - 2]])] for side in rows)
        rows = gather_step(block, rows, n, me)
    gathered = join(video[0], rows, me)
    query = jnp.dot(gathered, w_query, preferred_element_type=F32).astype(BF16)
    per = heads // chunks
    grad = after(cotangent[0], rows[0][-1], rows[1][-1], *pieces[1:])
    cots = gather_step(grad, ([], []), n, me)
    attention = []
    for c in range(chunks):
        source = after(query, cots[0][0], cots[1][0]) if c else query
        attention.append(attend(table, source, pieces, scale, c * per, per))
    attention = jnp.concatenate(attention, axis=1)
    partial = split(jnp.dot(attention, w_out, preferred_element_type=F32), n)
    for s in range(2, n):
        if s == n - 1:
            partial = [after(p, cots[0][-1], cots[1][-1]) for p in partial]
        cots = gather_step(grad, cots, n, me)
    grad_rows = join(grad, cots, me)
    sums, marks = (0, None, None), []
    for _ in range(1, n):
        sums = scatter_step(partial, sums, n, me)
        marks.append(sums[1:])
    output = (partial[0] + sums[1].astype(F32) + sums[2].astype(F32)).astype(BF16)
    grad_rows = after(grad_rows, *marks[0])

    grad_wo = contract_first(attention, grad_rows).astype(BF16)
    grad_attention = after(contract_last(grad_rows, w_out).astype(BF16), grad_wo, *marks[-2])
    sum_wo = ClipSum(grad_wo, [masks, masks[:1] + masks[:0:-1]])
    source = lax.rem(me - jnp.arange(n, dtype=jnp.int32) + n, n)
    back = attend_back(table, source, query, grad_attention, pieces, scale, 0, per)
    grad_attention = after(grad_attention, *sum_wo.step())
    for c in range(1, chunks):
        back = attend_back(table, source, query, grad_attention, pieces, scale, c * per, per, back)
    grad_query, grad_kv = back
    grad_kv = lax.all_to_all(grad_kv, "seq", split_axis=0, concat_axis=0, tiled=True)
    grad_ref = jnp.concatenate([grad_kv[k] for k in range(n)], axis=2)
    grad_wq = contract_first(gathered, grad_query).astype(BF16)
    sum_wq = ClipSum(grad_wq, [masks, masks[:1] + masks[:0:-1]])
    grad_query = after(grad_query, grad_wq)
    sum_wq.step()
    sum_wq.step(output)
    parts = split(contract_last(grad_query, w_query).astype(BF16), n)
    sums = (0, None, None)
    for s in range(1, n):
        if s == 2:
            parts = [after(p, grad_kv) for p in parts]
        sums = scatter_step(parts, sums, n, me)
        if s == 1:
            sum_wq.step(*sums[1:])
    grad_video = (parts[0] + sums[1].astype(F32) + sums[2].astype(F32)).astype(BF16)
    return (output[None], grad_video[None], sum_wq.result(), sum_wo.result(), grad_ref[None])


def solution(mesh):
    in_specs = (
        P("dp", "seq", None),
        P("dp", "seq", None),
        P(None, "seq"),
        P("seq", None),
        P("dp", None, "seq", None),
        P("dp", None, None, None),
    )
    out_specs = (
        P("dp", "seq", None),
        P("dp", "seq", None),
        P(None, "seq"),
        P("seq", None),
        P("dp", None, "seq", None),
    )
    return jax.shard_map(body, mesh=mesh, in_specs=in_specs, out_specs=out_specs, check_vma=False)
```

```python
import functools
import math

import jax
import jax.numpy as jnp
from jax import lax
from jax.experimental import pallas as pl
from jax.experimental.pallas import tpu as pltpu
from jax.sharding import PartitionSpec as P

HD = 128
TILE = 128
F32 = jnp.float32
BF16 = jnp.bfloat16
NEG = -1e30


def contract_last(left, right):
    return lax.dot_general(left, right, (((1,), (1,)), ((), ())), preferred_element_type=F32)


def contract_first(left, right):
    return lax.dot_general(left, right, (((0,), (0,)), ((), ())), preferred_element_type=F32)


def tile_table(tile_lists, ref_tiles, me, n):
    matched = jnp.any(tile_lists[..., None] == jnp.arange(ref_tiles, dtype=jnp.int32), axis=-2)
    table = jnp.transpose(matched, (1, 0, 2)).reshape(matched.shape[1], -1).astype(jnp.int32)
    source = lax.rem(me - jnp.arange(n, dtype=jnp.int32) + n, n)
    table = table.reshape(n, -1, table.shape[1])[source].reshape(table.shape)
    return table.reshape(table.shape[0], n, -1)[:, source].reshape(table.shape)


def masked(scores, table_ref, row, first, scale, axis):
    tiles = []
    for t in range(scores.shape[axis] // TILE):
        part = lax.slice_in_dim(scores, t * TILE, (t + 1) * TILE, axis=axis) * scale
        tiles.append(jnp.where(table_ref[row, first + t] != 0, part, NEG))
    return tiles


def forward_kernel(n, scale, table_ref, q_ref, *refs):
    kv_refs, out_ref = refs[:n], refs[n]
    local = kv_refs[0].shape[1] // TILE
    wide = math.gcd(q_ref.shape[0] // TILE, 4)

    def block(i, carry):
        rows = pl.ds(pl.multiple_of(i * wide * TILE, TILE), wide * TILE)
        query = q_ref[rows, :]
        scores = []
        for k in range(n):
            part = contract_last(kv_refs[k][0], query)
            for t in range(local):
                tiles = []
                for j in range(wide):
                    tile = part[t * TILE : (t + 1) * TILE, j * TILE : (j + 1) * TILE] * scale
                    tiles.append(jnp.where(table_ref[i * wide + j, k * local + t] != 0, tile, NEG))
                scores.append(jnp.concatenate(tiles, axis=1))
        peak = jnp.max(functools.reduce(jnp.maximum, scores), axis=0, keepdims=True)
        powers = [jnp.exp(s - peak) for s in scores]
        total = jnp.sum(functools.reduce(jnp.add, powers), axis=0, keepdims=True)
        inverse = 1.0 / total
        probs = [(p * inverse).astype(BF16) for p in powers]
        acc = None
        for k in range(n):
            part = jnp.concatenate(probs[k * local : (k + 1) * local], axis=0)
            part = contract_first(kv_refs[k][1], part)
            acc = part if acc is None else acc + part
        out_ref[rows, :] = acc.T.astype(BF16)
        return carry

    lax.fori_loop(0, q_ref.shape[0] // TILE // wide, block, 0)


def backward_kernel(n, scale, table_ref, source_ref, q_ref, g_ref, *refs):
    kv_refs, (dq_ref, dkv_ref, probs_ref, dscores_ref) = refs[:n], refs[-4:]
    length = kv_refs[0].shape[1]
    local = length // TILE

    wide = math.gcd(q_ref.shape[0] // TILE, 4)

    def block(i, carry):
        rows = pl.ds(pl.multiple_of(i * wide * TILE, TILE), wide * TILE)
        query, grad = q_ref[rows, :], g_ref[rows, :]
        scores, dprobs = [], []
        for k in range(n):
            part = contract_last(kv_refs[k][0], query)
            for t in range(local):
                tiles = []
                for j in range(wide):
                    tile = part[t * TILE : (t + 1) * TILE, j * TILE : (j + 1) * TILE] * scale
                    tiles.append(jnp.where(table_ref[i * wide + j, k * local + t] != 0, tile, NEG))
                scores.append(jnp.concatenate(tiles, axis=1))
        peak = functools.reduce(jnp.maximum, scores)
        peak = jnp.max(peak, axis=0, keepdims=True)
        powers = [jnp.exp(s - peak) for s in scores]
        total = jnp.sum(functools.reduce(jnp.add, powers), axis=0, keepdims=True)
        inverse = 1.0 / total
        weights = [p * inverse for p in powers]
        for k in range(n):
            part = contract_last(kv_refs[k][1], grad)
            dprobs += [part[t * TILE : (t + 1) * TILE] for t in range(local)]
        delta = functools.reduce(jnp.add, [d * w for d, w in zip(dprobs, weights)])
        delta = jnp.sum(delta, axis=0, keepdims=True)
        for j in range(n * local):
            keys = pl.ds(j * TILE, TILE)
            probs_ref[keys, rows] = weights[j].astype(BF16)
            dscores_ref[keys, rows] = (weights[j] * (dprobs[j] - delta) * scale).astype(BF16)
        return carry

    lax.fori_loop(0, q_ref.shape[0] // TILE // wide, block, 0)
    dq = None
    for k in range(n):
        keys = pl.ds(k * length, length)
        dscores = dscores_ref[keys, :]
        dkv_ref[source_ref[k], 0] = jnp.dot(dscores, q_ref[...], preferred_element_type=F32).astype(BF16)
        dkv_ref[source_ref[k], 1] = jnp.dot(probs_ref[keys, :], g_ref[...], preferred_element_type=F32).astype(BF16)
        part = contract_first(kv_refs[k][0], dscores)
        dq = part if dq is None else dq + part
    dq_ref[...] = dq.T.astype(BF16)


def attend(table, query, pieces, scale, first, heads):
    n = len(pieces)
    tokens = query.shape[0]
    width = heads * HD
    length = pieces[0].shape[1]
    rows = pl.BlockSpec((tokens, HD), lambda h, t: (0, first + h))
    piece = pl.BlockSpec((2, length, HD), lambda h, t: (0, 0, first + h))
    work = tokens * n * length * width
    return pl.pallas_call(
        functools.partial(forward_kernel, n, scale),
        out_shape=jax.ShapeDtypeStruct((tokens, width), BF16),
        grid_spec=pltpu.PrefetchScalarGridSpec(
            num_scalar_prefetch=1,
            grid=(heads,),
            in_specs=[rows] + [piece] * n,
            out_specs=pl.BlockSpec((tokens, HD), lambda h, t: (0, h)),
        ),
        cost_estimate=pl.CostEstimate(
            flops=4 * work, transcendentals=work // HD, bytes_accessed=4 * width * (tokens + n * length)
        ),
        compiler_params=pltpu.CompilerParams(vmem_limit_bytes=48 << 20),
    )(table, query, *pieces)


def attend_back(table, source, query, grad, pieces, scale, first, heads, earlier=()):
    n = len(pieces)
    tokens, width = query.shape
    length = pieces[0].shape[1]
    rows = pl.BlockSpec((tokens, HD), lambda h, t, s: (0, first + h))
    piece = pl.BlockSpec((2, length, HD), lambda h, t, s: (0, 0, first + h))
    work = tokens * n * length * heads * HD
    return pl.pallas_call(
        functools.partial(backward_kernel, n, scale),
        out_shape=[
            jax.ShapeDtypeStruct((tokens, width), BF16),
            jax.ShapeDtypeStruct((n, 2, length, width), BF16),
        ],
        grid_spec=pltpu.PrefetchScalarGridSpec(
            num_scalar_prefetch=2,
            grid=(heads,),
            in_specs=[rows, rows] + [piece] * n + [pl.BlockSpec(memory_space=pl.ANY)] * len(earlier),
            out_specs=[rows, pl.BlockSpec((n, 2, length, HD), lambda h, t, s: (0, 0, 0, first + h))],
            scratch_shapes=[pltpu.VMEM((n * length, tokens), BF16)] * 2,
        ),
        input_output_aliases={4 + n + i: i for i in range(len(earlier))},
        cost_estimate=pl.CostEstimate(
            flops=10 * work,
            transcendentals=work // HD,
            bytes_accessed=2 * heads * HD * (3 * tokens + 4 * n * length),
        ),
        compiler_params=pltpu.CompilerParams(vmem_limit_bytes=48 << 20),
    )(table, source, query, grad, *pieces, *earlier)


def after(array, *others):
    return lax.optimization_barrier((array, *others))[0]


def shift(array, n, by):
    return lax.ppermute(array, "seq", [(i, (i + by) % n) for i in range(n)])


def both_ways(right, left, ups, downs, me):
    up, down = [(i, i + 1) for i in ups], [(i, i - 1) for i in downs]
    apart = not {i for i, _ in up} & {i for i, _ in down} and not {j for _, j in up} & {j for _, j in down}
    if not apart:
        return lax.ppermute(right, "seq", up), lax.ppermute(left, "seq", down)
    rightward = (me >= ups[0]) & (me <= ups[-1])
    came = lax.ppermute(jnp.where(rightward, right, left), "seq", up + down)
    none = jnp.zeros_like(came)
    from_left = (me > ups[0]) & (me <= ups[-1] + 1)
    from_right = (me >= downs[0] - 1) & (me < downs[-1])
    return jnp.where(from_left, came, none), jnp.where(from_right, came, none)


def gather_step(block, state, n, me):
    s = len(state[0]) + 1
    right, left = (side[-1] if side else block for side in state)
    right, left = both_ways(right, left, range(s - 1, n - 1), range(1, n - s + 1), me)
    return (state[0] + [right], state[1] + [left])


def join(block, state, me):
    right, left = state
    others = [jnp.where(me > k, right[k], left[len(left) - 1 - k]) for k in range(len(right))]
    return jnp.concatenate([block] + others, axis=0)


def scatter_step(parts, state, n, me):
    steps, right, left = state
    s = steps + 1
    right = parts[s] if right is None else parts[s] + right.astype(F32)
    left = parts[n - s] if left is None else parts[n - s] + left.astype(F32)
    return s, *both_ways(right.astype(BF16), left.astype(BF16), range(s), range(n - s, n), me)


def split(partial, n):
    size = partial.shape[0] // n
    return [partial[k * size : (k + 1) * size].astype(F32) for k in range(n)]


class ClipSum:
    def __init__(self, array, paths):
        self.size = lax.axis_size("dp")
        self.index = lax.axis_index("dp")
        rows = array.shape[0] // len(paths)
        self.blocks = [array[p * rows : (p + 1) * rows] for p in range(len(paths))]
        self.paths = paths
        self.done = 0

    def exchange(self, block, mask):
        return lax.ppermute(block, "dp", [(i, i ^ mask) for i in range(self.size)])

    def step(self, *others):
        count = len(self.paths[0])
        if self.done == 2 * count:
            return ()
        for p, path in enumerate(self.paths):
            block = self.blocks[p]
            if self.done < count:
                mask = path[self.done]
                high = lax.shift_right_logical(self.index, mask.bit_length() - 1) & 1
                half = block.shape[0] // 2
                give = lax.dynamic_slice_in_dim(block, (1 - high) * half, half).astype(BF16)
                keep = lax.dynamic_slice_in_dim(block, high * half, half).astype(F32)
                self.blocks[p] = keep + self.exchange(after(give, *others), mask).astype(F32)
            else:
                mask = path[2 * count - 1 - self.done]
                high = lax.shift_right_logical(self.index, mask.bit_length() - 1) & 1
                block = after(block.astype(BF16), *others)
                other = self.exchange(block, mask)
                pair = jnp.concatenate([block, other]), jnp.concatenate([other, block])
                self.blocks[p] = jnp.where(high == 0, *pair)
        self.done += 1
        return tuple(self.blocks)

    def result(self):
        while self.done < 2 * len(self.paths[0]):
            self.step()
        return jnp.concatenate(self.blocks).astype(F32)


def body(video, cotangent, w_query, w_out, ref_kv, tile_lists):
    n = lax.axis_size("seq")
    me = lax.axis_index("seq")
    masks = [1 << b for b in range(lax.axis_size("dp").bit_length() - 1)]
    width = w_query.shape[1]
    heads = width // HD
    chunks = 2 if heads % 2 == 0 else 1
    length = ref_kv.shape[2]
    ref_tiles = length * n // TILE // tile_lists.shape[1]
    scale = 1.0 / math.sqrt(HD)
    table = tile_table(tile_lists[0], ref_tiles, me, n)

    pieces = []
    for k in range(n):
        columns = lax.rem(me + k, n) * width
        piece = lax.dynamic_slice_in_dim(ref_kv[0], columns, width, axis=2)
        pieces.append(shift(piece, n, k) if k else piece)
    order = sorted(range(1, n), key=lambda k: (min(k, n - k), -k))
    rows = ([], [])
    for s in range(1, n):
        block = video[0]
        if s > 1:
            rows = tuple(side[:-1] + [after(side[-1], pieces[order[s - 2]])] for side in rows)
        rows = gather_step(block, rows, n, me)
    gathered = join(video[0], rows, me)
    query = jnp.dot(gathered, w_query, preferred_element_type=F32).astype(BF16)
    per = heads // chunks
    grad = after(cotangent[0], rows[0][-2], rows[1][-2], *[pieces[k] for k in order[:-1]])
    cots = gather_step(grad, ([], []), n, me)
    attention = []
    for c in range(chunks):
        source = after(query, cots[0][0], cots[1][0]) if c else query
        attention.append(attend(table, source, pieces, scale, c * per, per))
    attention = jnp.concatenate(attention, axis=1)
    partial = split(jnp.dot(attention, w_out, preferred_element_type=F32), n)
    for s in range(2, n):
        if s == n - 1:
            partial = [after(p, cots[0][-1], cots[1][-1]) for p in partial]
        cots = gather_step(grad, cots, n, me)
    grad_rows = join(grad, cots, me)
    sums, marks = (0, None, None), []
    for _ in range(1, n):
        sums = scatter_step(partial, sums, n, me)
        marks.append(sums[1:])
    output = (partial[0] + sums[1].astype(F32) + sums[2].astype(F32)).astype(BF16)
    grad_rows = after(grad_rows, *marks[0])

    grad_wo = contract_first(attention, grad_rows).astype(BF16)
    grad_attention = after(contract_last(grad_rows, w_out).astype(BF16), grad_wo)
    sum_wo = ClipSum(grad_wo, [masks, masks[:1] + masks[:0:-1]])
    source = lax.rem(me - jnp.arange(n, dtype=jnp.int32) + n, n)
    back = attend_back(table, source, query, grad_attention, pieces, scale, 0, per)
    grad_attention = after(grad_attention, *sum_wo.step(), *marks[-2])
    for c in range(1, chunks):
        back = attend_back(table, source, query, grad_attention, pieces, scale, c * per, per, back)
    grad_query, grad_kv = back
    grad_kv = lax.all_to_all(grad_kv, "seq", split_axis=0, concat_axis=0, tiled=True)
    grad_ref = jnp.concatenate([grad_kv[k] for k in range(n)], axis=2)
    grad_wq = contract_first(gathered, grad_query).astype(BF16)
    sum_wq = ClipSum(grad_wq, [masks, masks[:1] + masks[:0:-1]])
    grad_query = after(grad_query, grad_wq)
    sum_wq.step()
    sum_wq.step(output)
    parts = split(contract_last(grad_query, w_query).astype(BF16), n)
    sums = (0, None, None)
    for s in range(1, n):
        if s == 2:
            parts = [after(p, grad_kv) for p in parts]
        sums = scatter_step(parts, sums, n, me)
        if s == 1:
            sum_wq.step(*sums[1:])
    weights = sum_wq.result(), sum_wo.result()
    last = after(parts[0], *weights)
    grad_video = (last + sums[1].astype(F32) + sums[2].astype(F32)).astype(BF16)
    return (output[None], grad_video[None], *weights, grad_ref[None])


def solution(mesh):
    in_specs = (
        P("dp", "seq", None),
        P("dp", "seq", None),
        P(None, "seq"),
        P("seq", None),
        P("dp", None, "seq", None),
        P("dp", None, None, None),
    )
    out_specs = (
        P("dp", "seq", None),
        P("dp", "seq", None),
        P(None, "seq"),
        P("seq", None),
        P("dp", None, "seq", None),
    )
    return jax.shard_map(body, mesh=mesh, in_specs=in_specs, out_specs=out_specs, check_vma=False)
```

```python
import functools
import math

import jax
import jax.numpy as jnp
from jax import lax
from jax.experimental import pallas as pl
from jax.experimental.pallas import tpu as pltpu
from jax.sharding import PartitionSpec as P

HD = 128
TILE = 128
F32 = jnp.float32
BF16 = jnp.bfloat16
NEG = -1e30


def contract_last(left, right):
    return lax.dot_general(left, right, (((1,), (1,)), ((), ())), preferred_element_type=F32)


def contract_first(left, right):
    return lax.dot_general(left, right, (((0,), (0,)), ((), ())), preferred_element_type=F32)


def tile_table(tile_lists, ref_tiles, me, n):
    matched = jnp.any(tile_lists[..., None] == jnp.arange(ref_tiles, dtype=jnp.int32), axis=-2)
    table = jnp.transpose(matched, (1, 0, 2)).reshape(matched.shape[1], -1).astype(jnp.int32)
    source = lax.rem(me - jnp.arange(n, dtype=jnp.int32) + n, n)
    table = table.reshape(n, -1, table.shape[1])[source].reshape(table.shape)
    return table.reshape(table.shape[0], n, -1)[:, source].reshape(table.shape)


def masked(scores, table_ref, row, first, scale, axis):
    tiles = []
    for t in range(scores.shape[axis] // TILE):
        part = lax.slice_in_dim(scores, t * TILE, (t + 1) * TILE, axis=axis) * scale
        tiles.append(jnp.where(table_ref[row, first + t] != 0, part, NEG))
    return tiles


def forward_kernel(n, scale, table_ref, q_ref, *refs):
    kv_refs, out_ref = refs[:n], refs[n]
    local = kv_refs[0].shape[1] // TILE
    wide = math.gcd(q_ref.shape[0] // TILE, 4)

    def block(i, carry):
        rows = pl.ds(pl.multiple_of(i * wide * TILE, TILE), wide * TILE)
        query = q_ref[rows, :]
        scores = []
        for k in range(n):
            part = contract_last(kv_refs[k][0], query)
            for t in range(local):
                tiles = []
                for j in range(wide):
                    tile = part[t * TILE : (t + 1) * TILE, j * TILE : (j + 1) * TILE] * scale
                    tiles.append(jnp.where(table_ref[i * wide + j, k * local + t] != 0, tile, NEG))
                scores.append(jnp.concatenate(tiles, axis=1))
        peak = jnp.max(functools.reduce(jnp.maximum, scores), axis=0, keepdims=True)
        powers = [jnp.exp(s - peak) for s in scores]
        total = jnp.sum(functools.reduce(jnp.add, powers), axis=0, keepdims=True)
        inverse = 1.0 / total
        probs = [(p * inverse).astype(BF16) for p in powers]
        acc = None
        for k in range(n):
            part = jnp.concatenate(probs[k * local : (k + 1) * local], axis=0)
            part = contract_first(kv_refs[k][1], part)
            acc = part if acc is None else acc + part
        out_ref[rows, :] = acc.T.astype(BF16)
        return carry

    lax.fori_loop(0, q_ref.shape[0] // TILE // wide, block, 0)


def backward_kernel(n, scale, table_ref, source_ref, q_ref, g_ref, *refs):
    kv_refs, (dq_ref, dkv_ref, probs_ref, dscores_ref) = refs[:n], refs[-4:]
    length = kv_refs[0].shape[1]
    local = length // TILE

    wide = math.gcd(q_ref.shape[0] // TILE, 4)

    def block(i, carry):
        rows = pl.ds(pl.multiple_of(i * wide * TILE, TILE), wide * TILE)
        query, grad = q_ref[rows, :], g_ref[rows, :]
        scores, dprobs = [], []
        for k in range(n):
            part = contract_last(kv_refs[k][0], query)
            for t in range(local):
                tiles = []
                for j in range(wide):
                    tile = part[t * TILE : (t + 1) * TILE, j * TILE : (j + 1) * TILE] * scale
                    tiles.append(jnp.where(table_ref[i * wide + j, k * local + t] != 0, tile, NEG))
                scores.append(jnp.concatenate(tiles, axis=1))
        peak = functools.reduce(jnp.maximum, scores)
        peak = jnp.max(peak, axis=0, keepdims=True)
        powers = [jnp.exp(s - peak) for s in scores]
        total = jnp.sum(functools.reduce(jnp.add, powers), axis=0, keepdims=True)
        inverse = 1.0 / total
        weights = [p * inverse for p in powers]
        for k in range(n):
            part = contract_last(kv_refs[k][1], grad)
            dprobs += [part[t * TILE : (t + 1) * TILE] for t in range(local)]
        delta = functools.reduce(jnp.add, [d * w for d, w in zip(dprobs, weights)])
        delta = jnp.sum(delta, axis=0, keepdims=True)
        for j in range(n * local):
            keys = pl.ds(j * TILE, TILE)
            probs_ref[keys, rows] = weights[j].astype(BF16)
            dscores_ref[keys, rows] = (weights[j] * (dprobs[j] - delta) * scale).astype(BF16)
        return carry

    lax.fori_loop(0, q_ref.shape[0] // TILE // wide, block, 0)
    dq = None
    for k in range(n):
        keys = pl.ds(k * length, length)
        dscores = dscores_ref[keys, :]
        dkv_ref[source_ref[k], 0] = jnp.dot(dscores, q_ref[...], preferred_element_type=F32).astype(BF16)
        dkv_ref[source_ref[k], 1] = jnp.dot(probs_ref[keys, :], g_ref[...], preferred_element_type=F32).astype(BF16)
        part = contract_first(kv_refs[k][0], dscores)
        dq = part if dq is None else dq + part
    dq_ref[...] = dq.T.astype(BF16)


def attend(table, query, pieces, scale, first, heads):
    n = len(pieces)
    tokens = query.shape[0]
    width = heads * HD
    length = pieces[0].shape[1]
    rows = pl.BlockSpec((tokens, HD), lambda h, t: (0, first + h))
    piece = pl.BlockSpec((2, length, HD), lambda h, t: (0, 0, first + h))
    work = tokens * n * length * width
    return pl.pallas_call(
        functools.partial(forward_kernel, n, scale),
        out_shape=jax.ShapeDtypeStruct((tokens, width), BF16),
        grid_spec=pltpu.PrefetchScalarGridSpec(
            num_scalar_prefetch=1,
            grid=(heads,),
            in_specs=[rows] + [piece] * n,
            out_specs=pl.BlockSpec((tokens, HD), lambda h, t: (0, h)),
        ),
        cost_estimate=pl.CostEstimate(
            flops=4 * work, transcendentals=work // HD, bytes_accessed=4 * width * (tokens + n * length)
        ),
        compiler_params=pltpu.CompilerParams(vmem_limit_bytes=48 << 20),
    )(table, query, *pieces)


def attend_back(table, source, query, grad, pieces, scale, first, heads, earlier=()):
    n = len(pieces)
    tokens, width = query.shape
    length = pieces[0].shape[1]
    rows = pl.BlockSpec((tokens, HD), lambda h, t, s: (0, first + h))
    piece = pl.BlockSpec((2, length, HD), lambda h, t, s: (0, 0, first + h))
    work = tokens * n * length * heads * HD
    return pl.pallas_call(
        functools.partial(backward_kernel, n, scale),
        out_shape=[
            jax.ShapeDtypeStruct((tokens, width), BF16),
            jax.ShapeDtypeStruct((n, 2, length, width), BF16),
        ],
        grid_spec=pltpu.PrefetchScalarGridSpec(
            num_scalar_prefetch=2,
            grid=(heads,),
            in_specs=[rows, rows] + [piece] * n + [pl.BlockSpec(memory_space=pl.ANY)] * len(earlier),
            out_specs=[rows, pl.BlockSpec((n, 2, length, HD), lambda h, t, s: (0, 0, 0, first + h))],
            scratch_shapes=[pltpu.VMEM((n * length, tokens), BF16)] * 2,
        ),
        input_output_aliases={4 + n + i: i for i in range(len(earlier))},
        cost_estimate=pl.CostEstimate(
            flops=10 * work,
            transcendentals=work // HD,
            bytes_accessed=2 * heads * HD * (3 * tokens + 4 * n * length),
        ),
        compiler_params=pltpu.CompilerParams(vmem_limit_bytes=48 << 20),
    )(table, source, query, grad, *pieces, *earlier)


def after(array, *others):
    return lax.optimization_barrier((array, *others))[0]


def shift(array, n, by):
    return lax.ppermute(array, "seq", [(i, (i + by) % n) for i in range(n)])


def both_ways(right, left, ups, downs, me):
    up, down = [(i, i + 1) for i in ups], [(i, i - 1) for i in downs]
    apart = not {i for i, _ in up} & {i for i, _ in down} and not {j for _, j in up} & {j for _, j in down}
    if not apart:
        return lax.ppermute(right, "seq", up), lax.ppermute(left, "seq", down)
    rightward = (me >= ups[0]) & (me <= ups[-1])
    came = lax.ppermute(jnp.where(rightward, right, left), "seq", up + down)
    none = jnp.zeros_like(came)
    from_left = (me > ups[0]) & (me <= ups[-1] + 1)
    from_right = (me >= downs[0] - 1) & (me < downs[-1])
    return jnp.where(from_left, came, none), jnp.where(from_right, came, none)


def gather_step(block, state, n, me):
    s = len(state[0]) + 1
    right, left = (side[-1] if side else block for side in state)
    right, left = both_ways(right, left, range(s - 1, n - 1), range(1, n - s + 1), me)
    return (state[0] + [right], state[1] + [left])


def join(block, state, me):
    right, left = state
    others = [jnp.where(me > k, right[k], left[len(left) - 1 - k]) for k in range(len(right))]
    return jnp.concatenate([block] + others, axis=0)


def scatter_step(parts, state, n, me):
    steps, right, left = state
    s = steps + 1
    right = parts[s] if right is None else parts[s] + right.astype(F32)
    left = parts[n - s] if left is None else parts[n - s] + left.astype(F32)
    return s, *both_ways(right.astype(BF16), left.astype(BF16), range(s), range(n - s, n), me)


def split(partial, n):
    size = partial.shape[0] // n
    return [partial[k * size : (k + 1) * size].astype(F32) for k in range(n)]


class ClipSum:
    def __init__(self, array, paths):
        self.size = lax.axis_size("dp")
        self.index = lax.axis_index("dp")
        rows = array.shape[0] // len(paths)
        self.blocks = [array[p * rows : (p + 1) * rows] for p in range(len(paths))]
        self.paths = paths
        self.done = 0

    def exchange(self, block, mask):
        return lax.ppermute(block, "dp", [(i, i ^ mask) for i in range(self.size)])

    def step(self, *others):
        count = len(self.paths[0])
        if self.done == 2 * count:
            return ()
        for p, path in enumerate(self.paths):
            block = self.blocks[p]
            if self.done < count:
                mask = path[self.done]
                high = lax.shift_right_logical(self.index, mask.bit_length() - 1) & 1
                half = block.shape[0] // 2
                give = lax.dynamic_slice_in_dim(block, (1 - high) * half, half).astype(BF16)
                keep = lax.dynamic_slice_in_dim(block, high * half, half).astype(F32)
                self.blocks[p] = keep + self.exchange(after(give, *others), mask).astype(F32)
            else:
                mask = path[2 * count - 1 - self.done]
                high = lax.shift_right_logical(self.index, mask.bit_length() - 1) & 1
                block = after(block.astype(BF16), *others)
                other = self.exchange(block, mask)
                pair = jnp.concatenate([block, other]), jnp.concatenate([other, block])
                self.blocks[p] = jnp.where(high == 0, *pair)
        self.done += 1
        return tuple(self.blocks)

    def result(self):
        while self.done < 2 * len(self.paths[0]):
            self.step()
        return jnp.concatenate(self.blocks).astype(F32)


def body(video, cotangent, w_query, w_out, ref_kv, tile_lists):
    n = lax.axis_size("seq")
    me = lax.axis_index("seq")
    masks = [1 << b for b in range(lax.axis_size("dp").bit_length() - 1)]
    width = w_query.shape[1]
    heads = width // HD
    chunks = 2 if heads % 2 == 0 else 1
    length = ref_kv.shape[2]
    ref_tiles = length * n // TILE // tile_lists.shape[1]
    scale = 1.0 / math.sqrt(HD)
    table = tile_table(tile_lists[0], ref_tiles, me, n)

    pieces = []
    for k in range(n):
        columns = lax.rem(me + k, n) * width
        piece = lax.dynamic_slice_in_dim(ref_kv[0], columns, width, axis=2)
        pieces.append(shift(piece, n, k) if k else piece)
    order = sorted(range(1, n), key=lambda k: (min(k, n - k), -k))
    rows = ([], [])
    for s in range(1, n):
        block = video[0]
        if s > 1:
            rows = tuple(side[:-1] + [after(side[-1], pieces[order[s - 2]])] for side in rows)
        rows = gather_step(block, rows, n, me)
    gathered = join(video[0], rows, me)
    query = jnp.dot(gathered, w_query, preferred_element_type=F32).astype(BF16)
    per = heads // chunks
    grad = after(cotangent[0], rows[0][-2], rows[1][-2], *[pieces[k] for k in order[:-1]])
    cots = gather_step(grad, ([], []), n, me)
    attention = []
    for c in range(chunks):
        source = after(query, cots[0][0], cots[1][0]) if c else query
        attention.append(attend(table, source, pieces, scale, c * per, per))
    attention = jnp.concatenate(attention, axis=1)
    partial = split(jnp.dot(attention, w_out, preferred_element_type=F32), n)
    for s in range(2, n):
        if s == n - 1:
            partial = [after(p, cots[0][-1], cots[1][-1]) for p in partial]
        cots = gather_step(grad, cots, n, me)
    grad_rows = join(grad, cots, me)
    sums, marks = (0, None, None), []
    for _ in range(1, n):
        sums = scatter_step(partial, sums, n, me)
        marks.append(sums[1:])
    output = (partial[0] + sums[1].astype(F32) + sums[2].astype(F32)).astype(BF16)
    grad_rows = after(grad_rows, *marks[0])

    grad_wo = contract_first(attention, grad_rows).astype(BF16)
    grad_attention = after(contract_last(grad_rows, w_out).astype(BF16), grad_wo)
    sum_wo = ClipSum(grad_wo, [masks, masks[:1] + masks[:0:-1]])
    source = lax.rem(me - jnp.arange(n, dtype=jnp.int32) + n, n)
    back = attend_back(table, source, query, grad_attention, pieces, scale, 0, per)
    grad_attention = after(grad_attention, *sum_wo.step())
    for c in range(1, chunks):
        back = attend_back(table, source, query, grad_attention, pieces, scale, c * per, per, back)
    grad_query, grad_kv = back
    grad_kv = lax.all_to_all(grad_kv, "seq", split_axis=0, concat_axis=0, tiled=True)
    grad_ref = jnp.concatenate([grad_kv[k] for k in range(n)], axis=2)
    grad_query = after(grad_query, *marks[-2])
    grad_wq = contract_first(gathered, grad_query).astype(BF16)
    sum_wq = ClipSum(grad_wq, [masks, masks[:1] + masks[:0:-1]])
    grad_query = after(grad_query, grad_wq)
    sum_wq.step()
    sum_wq.step(output)
    parts = split(contract_last(grad_query, w_query).astype(BF16), n)
    sums = (0, None, None)
    for s in range(1, n):
        if s == 2:
            parts = [after(p, grad_kv) for p in parts]
        sums = scatter_step(parts, sums, n, me)
        if s == 1:
            sum_wq.step(*sums[1:])
    weights = sum_wq.result(), sum_wo.result()
    last = after(parts[0], *weights)
    grad_video = (last + sums[1].astype(F32) + sums[2].astype(F32)).astype(BF16)
    return (output[None], grad_video[None], *weights, grad_ref[None])


def solution(mesh):
    in_specs = (
        P("dp", "seq", None),
        P("dp", "seq", None),
        P(None, "seq"),
        P("seq", None),
        P("dp", None, "seq", None),
        P("dp", None, None, None),
    )
    out_specs = (
        P("dp", "seq", None),
        P("dp", "seq", None),
        P(None, "seq"),
        P("seq", None),
        P("dp", None, "seq", None),
    )
    return jax.shard_map(body, mesh=mesh, in_specs=in_specs, out_specs=out_specs, check_vma=False)
```
